256 devices in a mesh: front: 64 (over x_lo, y, z), pair: 4 (over x_hi, core).
Axes of the slice: x: 4 (x_hi: 2, x_lo: 2; x = x_hi * 2 + x_lo), y: 4, z: 8, core: 2. Of those that a mesh axis runs over, the one named last changes fastest.
Arguments:
- pivot_block: float32 [64, 768, 768], P('front', 'pair'), may hold values from -1 to 8, as said below
- coupling_rows: float32 [64, 2304, 768], P('front', 'pair'), may hold values from -0.6 to 0.6
- trailing_block: float32 [64, 2304, 2304], P('front', 'pair'), may hold values from -6 to 6
- index_map: int32 [64, 2304], replicated, may hold values from 0 to 3071, as said below
Outputs:
- panel_factor: float32 [64, 2304, 768], P('front', 'pair')
- parent_front: float32 [3072, 64, 768], P('pair', 'front')
The draws below stay inside these ranges and needn't reach their ends.
Inputs may be any that keep to these rules, and one draw needn't show every extreme that they name: pivot_block[c] is symmetric positive definite. For each child c and row block p, the entries index_map[c, p * 576 + a] for a below 576 are distinct, rising, and lie in p * 768 to (p + 1) * 768 - 1.
All inputs are finite; a program needn't handle non-finite values.
Results may differ from the reference program's by a relative error of at most 0.0029.
Values may be sent and summed in bfloat16 or wider, within the bound.
No kernel may reach another device: no remote copies, remote signals or barrier semaphores. Data moves between devices by JAX's collectives and lax.ppermute only.
A program may use at most 128 MiB of HBM per device.

```python
import jax
import jax.numpy as jnp
from jax import lax

PIV = 768
UPD = 2304
PO = 3072
CHILDREN = 64
PARENTS = 16
UPD_BLK = 576
PAR_BLK = 768


def draw_pivot_block(key, part):
    first_key, second_key = jax.random.split(jax.random.fold_in(key, 11))
    normals = jax.random.normal(first_key, (CHILDREN, PIV, PIV), jnp.float32)
    gram = jnp.einsum('cik,cjk->cij', normals, normals) / PIV
    lifted = jax.random.uniform(second_key, (CHILDREN, PIV), jnp.float32, 1.0, 2.0)
    return gram + lifted[:, :, None] * jnp.eye(PIV, dtype=jnp.float32)[None, :, :]


def draw_index_map(key, part):
    blocks = PO // PAR_BLK
    keys = jax.random.split(jax.random.fold_in(key, 7), CHILDREN * blocks)
    picks = jax.vmap(lambda one_key: jnp.sort(jax.random.permutation(one_key, PAR_BLK)[:UPD_BLK]))(keys)
    offsets = jnp.arange(CHILDREN * blocks, dtype=jnp.int32) % blocks * PAR_BLK
    return (picks.astype(jnp.int32) + offsets[:, None]).reshape(CHILDREN, UPD).astype(jnp.int32)


def block_levels(own_key, shape, cuts, smallest, top_value):
    def one(axis_at, shards_of):
        steps = jax.random.uniform(jax.random.fold_in(jax.random.fold_in(own_key, 6), axis_at), (shards_of,), jnp.float32, smallest / len(cuts), top_value / len(cuts))
        return jnp.repeat(jnp.exp(steps), shape[axis_at] // shards_of).reshape((-1,) + (1,) * (len(shape) - axis_at - 1))

    factor_of = one(*cuts[0])
    for cut in cuts[1:]:
        factor_of = factor_of * one(*cut)
    return factor_of


def bell_draw(stream_key, extent, spread, most, cuts=(), kind=jnp.bfloat16):
    result = spread * jax.random.normal(stream_key, extent, jnp.float32)
    if cuts:
        result = result * block_levels(stream_key, extent, cuts, -0.22, 0.18)
    return jnp.clip(result, -most, most).astype(kind)


def setup_inputs(seed: int = 0) -> dict:
    key_list = jax.random.split(jax.random.key(seed), 5)
    return {
        "pivot_block": draw_pivot_block(jax.random.fold_in(key_list[4], 71), 0),
        "coupling_rows": bell_draw(key_list[1], (CHILDREN, UPD, PIV), 0.1, 0.6, ((0, 64), (1, 4)), jnp.float32),
        "trailing_block": bell_draw(key_list[2], (CHILDREN, UPD, UPD), 1.0, 6.0, ((0, 64), (1, 4)), jnp.float32),
        "index_map": draw_index_map(jax.random.fold_in(key_list[4], 71), 0),
    }


def eliminate(pivot, coupling, trailing):
    lower_factor = jnp.linalg.cholesky(pivot)
    factor = jax.scipy.linalg.solve_triangular(lower_factor, coupling.T, lower=True).T
    rounded = lax.optimization_barrier(factor.astype(jnp.bfloat16))
    panel_half = rounded.astype(jnp.float32)
    product = jnp.dot(panel_half, panel_half.T, precision=lax.Precision.HIGHEST)
    return (factor, (trailing - product).astype(jnp.bfloat16))

def assemble(group):
    pivots, couplings, trailings, maps = group
    front_sum = jnp.zeros((PO, PO), jnp.float32)
    factors = []
    for member in range(4):
        factor, update = eliminate(pivots[member], couplings[member], trailings[member])
        rows_map = maps[member].astype(jnp.int32)
        front_sum = front_sum.at[rows_map[:, None], rows_map[None, :]].add(update.astype(jnp.float32))
        factors.append(factor)
    return (jnp.stack(factors), front_sum)

def reference(pivot_block, coupling_rows, trailing_block, index_map):
    groups = (pivot_block.reshape(PARENTS, 4, PIV, PIV), coupling_rows.reshape(PARENTS, 4, UPD, PIV), trailing_block.reshape(PARENTS, 4, UPD, UPD), index_map.reshape(PARENTS, 4, UPD))
    factors, fronts = lax.map(assemble, groups)
    panel_factor = factors.reshape(CHILDREN, UPD, PIV)
    parent_front = fronts.reshape(PARENTS, PO, 4, PO // 4).transpose(1, 0, 2, 3).reshape(PO, 4 * PARENTS, PO // 4)
    return (panel_factor, parent_front)
```

```python
import jax
import jax.numpy as jnp
from jax import lax
from jax.sharding import PartitionSpec as P

PO = 3072


def xor_permute(value, axis, bits):
    return lax.ppermute(value, axis, [(i, i ^ bits) for i in range(lax.axis_size(axis))])


def gather_pair(block, pair_id):
    rows = block.shape[0]
    size = lax.axis_size("pair")
    far = xor_permute(block, "pair", 2)
    near = xor_permute(block, "pair", 1)
    cross = xor_permute(far, "pair", 1)
    whole = jnp.zeros((size * rows,) + block.shape[1:], block.dtype)
    for bits, part in enumerate((block, near, far, cross)):
        whole = lax.dynamic_update_slice_in_dim(whole, part, (pair_id ^ bits) * rows, 0)
    return whole


def body(pivot_block, coupling_rows, trailing_block, index_map):
    child_id = lax.axis_index("front")
    pair_id = lax.axis_index("pair")
    pairs = lax.axis_size("pair")
    sibling = child_id % 4
    upd_rows = coupling_rows.shape[1]
    par_rows = PO // pairs
    whole_pivot = gather_pair(pivot_block[0], pair_id)
    lower_factor = jnp.linalg.cholesky(whole_pivot)
    factor = jax.scipy.linalg.solve_triangular(lower_factor, coupling_rows[0].T, lower=True).T
    panel_half = factor.astype(jnp.bfloat16)
    whole_panel = gather_pair(panel_half, pair_id)
    product = lax.dot_general(
        panel_half, whole_panel, (((1,), (1,)), ((), ())), preferred_element_type=jnp.float32
    )
    update = (trailing_block[0] - product).astype(jnp.bfloat16)

    def column_block(which):
        return lax.dynamic_slice_in_dim(update, which * upd_rows, upd_rows, 1)

    def hot(which, block):
        child_map = lax.dynamic_slice(index_map, (which, block * upd_rows), (1, upd_rows))[0]
        local = child_map - block * par_rows
        return (local[None, :] == jnp.arange(par_rows, dtype=jnp.int32)[:, None]).astype(
            jnp.bfloat16
        )

    assembled = jnp.zeros((par_rows, par_rows), jnp.float32)
    parts = [column_block(sibling)]
    for bits in (1, 2, 3):
        parts.append(xor_permute(column_block(sibling ^ bits), "front", bits))
    for bits, part in enumerate(parts):
        which = child_id ^ bits
        moved = jnp.dot(hot(which, pair_id), part, preferred_element_type=jnp.float32)
        assembled = assembled + lax.dot_general(
            moved.astype(jnp.bfloat16),
            hot(which, sibling),
            (((1,), (1,)), ((), ())),
            preferred_element_type=jnp.float32,
        )
    return (factor[None, :, :], assembled[:, None, :])


def solution(mesh):
    in_specs = (P("front", "pair", None), P("front", "pair", None), P("front", "pair", None), P())
    out_specs = (P("front", "pair", None), P("pair", "front", None))
    return jax.shard_map(body, mesh=mesh, in_specs=in_specs, out_specs=out_specs, check_vma=False)
```

```python
import functools

import jax
import jax.numpy as jnp
from jax import lax
from jax.experimental import pallas as pl
from jax.experimental.pallas import tpu as pltpu
from jax.sharding import PartitionSpec as P

PO = 3072
LEAF = 128
F32 = jnp.float32
BF16 = jnp.bfloat16


def xor_permute(value, axis, bits):
    return lax.ppermute(value, axis, [(i, i ^ bits) for i in range(lax.axis_size(axis))])


def gather_pair(block):
    far = xor_permute(block, "pair", 2)
    near = xor_permute(block, "pair", 1)
    cross = xor_permute(far, "pair", 1)
    return block, near, far, cross


def lane_wide(value, lane):
    return jnp.broadcast_to(value[:, lane : lane + 1], (8, LEAF))


def row_wide(value, row):
    return jnp.broadcast_to(value[row : row + 1, :], (8, LEAF))


def eliminate(groups, lane0, sub):
    diag, unit = groups[0]
    cols = [lane_wide(diag, lane0 + k) for k in range(8)]
    below = [[lane_wide(group[0], lane0 + k) for k in range(8)] for group in groups[1:]]
    rest = list(groups[1:])
    scale = None
    for k in range(8):
        pivot = row_wide(cols[k], k)
        inverse = 1.0 / pivot
        root = lax.rsqrt(pivot)
        scale = root if scale is None else jnp.where(sub == k, root, scale)
        diag_row, unit_row = row_wide(diag, k), row_wide(unit, k)
        factor = jnp.where(sub > k, cols[k] * inverse, 0.0)
        others = [one[k] * inverse for one in below]
        for m in range(k + 1, 8):
            entry = row_wide(cols[m], k)
            cols[m] = cols[m] - factor * entry
            for one, other in zip(below, others):
                one[m] = one[m] - other * entry
        diag = diag - factor * diag_row
        unit = unit - factor * unit_row
        rest = [
            (one - other * diag_row, two - other * unit_row)
            for (one, two), other in zip(rest, others)
        ]
    return diag * scale, unit * scale, rest


def factor_leaf(d_ref, x_ref):
    sub = lax.broadcasted_iota(jnp.int32, (8, LEAF), 0)
    x_ref[...] = (
        lax.broadcasted_iota(jnp.int32, (LEAF, LEAF), 0)
        == lax.broadcasted_iota(jnp.int32, (LEAF, LEAF), 1)
    ).astype(F32)
    for start in range(0, LEAF, 32):
        groups = [
            (d_ref[start + g : start + g + 8, :], x_ref[start + g : start + g + 8, :])
            for g in range(0, 32, 8)
        ]
        uppers, inverses = [], []
        for g in range(0, 32, 8):
            upper, inverse, groups = eliminate(groups, start + g, sub)
            uppers.append(upper)
            inverses.append(inverse)
        upper, inverse = jnp.concatenate(uppers, 0), jnp.concatenate(inverses, 0)
        x_ref[start : start + 32, :] = inverse
        row = start + 32
        if row < LEAF:
            change = lax.dot_general(
                upper,
                jnp.concatenate([upper, inverse], 1),
                (((0,), (0,)), ((), ())),
                precision=lax.Precision.HIGHEST,
                preferred_element_type=F32,
            )
            d_ref[row:, :] = d_ref[row:, :] - change[row:, :LEAF]
            x_ref[row:, :] = x_ref[row:, :] - change[row:, LEAF:]


def halves(value):
    high = value.astype(BF16)
    return high, (value - high.astype(F32)).astype(BF16)


def left_three(value):
    high, low = halves(value)
    return jnp.concatenate([high, high, low], 1)


def right_three(value):
    high, low = halves(value)
    return jnp.concatenate([high, low, high], 0)


def mxu(left, right):
    return jnp.dot(left, right, preferred_element_type=F32)


def factor_kernel(p0, p1, p2, p3, c_ref, f_ref, h_ref, a_ref, w_ref, d_ref, x_ref, l_ref, r_ref):
    pair_id = lax.axis_index("pair")
    rows = p0.shape[0]
    blocks = p0.shape[1] // LEAF
    for bits, part in enumerate((p0, p1, p2, p3)):
        at = pl.multiple_of((pair_id ^ bits) * rows, 64)
        for j in range(blocks):
            a_ref[j, pl.ds(at, rows), :] = part[:, j * LEAF : (j + 1) * LEAF]
    for j in range(blocks):
        w_ref[j] = c_ref[:, j * LEAF : (j + 1) * LEAF]

    def step(k, _):
        here = pl.ds(pl.multiple_of(k * LEAF, LEAF), LEAF)
        d_ref[...] = a_ref[k, here, :]
        factor_leaf(d_ref, x_ref)
        inverse = x_ref[...]
        spread = left_three(inverse)
        panel = mxu(left_three(w_ref[k]), right_three(inverse.T))
        w_ref[k] = panel
        panel3 = left_three(panel)

        def row(j, _):
            upper = mxu(spread, right_three(a_ref[j, here, :]))
            l_ref[j] = left_three(upper.T)
            r_ref[j] = right_three(upper)
            w_ref[j] = w_ref[j] - mxu(panel3, r_ref[j])
            return 0

        lax.fori_loop(k + 1, blocks, row, 0)

        def trail(i, _):
            there = pl.ds(pl.multiple_of(i * LEAF, LEAF), LEAF)

            def one(j, _):
                a_ref[j, there, :] = a_ref[j, there, :] - mxu(l_ref[i], r_ref[j])
                return 0

            lax.fori_loop(i, blocks, one, 0)
            return 0

        lax.fori_loop(k + 1, blocks, trail, 0)
        return 0

    lax.fori_loop(0, blocks, step, 0)
    for j in range(blocks):
        f_ref[:, j * LEAF : (j + 1) * LEAF] = w_ref[j]
        h_ref[:, j * LEAF : (j + 1) * LEAF] = w_ref[j].astype(BF16)


def factor_panel(parts, coupling):
    upd_rows, piv = coupling.shape
    blocks = piv // LEAF
    return pl.pallas_call(
        factor_kernel,
        out_shape=(
            jax.ShapeDtypeStruct((upd_rows, piv), F32),
            jax.ShapeDtypeStruct((upd_rows, piv), BF16),
        ),
        scratch_shapes=[
            pltpu.VMEM((blocks, piv, LEAF), F32),
            pltpu.VMEM((blocks, upd_rows, LEAF), F32),
            pltpu.VMEM((LEAF, LEAF), F32),
            pltpu.VMEM((LEAF, LEAF), F32),
            pltpu.VMEM((blocks, LEAF, 3 * LEAF), BF16),
            pltpu.VMEM((blocks, 3 * LEAF, LEAF), BF16),
        ],
        compiler_params=pltpu.CompilerParams(vmem_limit_bytes=48 << 20),
    )(*parts, coupling)


def body(pivot_block, coupling_rows, trailing_block, index_map):
    child_id = lax.axis_index("front")
    pair_id = lax.axis_index("pair")
    pairs = lax.axis_size("pair")
    sibling = child_id % 4
    upd_rows = coupling_rows.shape[1]
    par_rows = PO // pairs
    factor, panel_half = factor_panel(gather_pair(pivot_block[0]), coupling_rows[0])
    panels = gather_pair(panel_half)

    def update_for(bits):
        column = sibling ^ bits
        panel = lax.select_n(column ^ pair_id, *panels)
        product = lax.dot_general(
            panel_half, panel, (((1,), (1,)), ((), ())), preferred_element_type=F32
        )
        trailing = lax.dynamic_slice_in_dim(trailing_block[0], column * upd_rows, upd_rows, 1)
        return (trailing - product).astype(BF16)

    def hot(which, block):
        child_map = lax.dynamic_slice(index_map, (which, block * upd_rows), (1, upd_rows))[0]
        local = child_map - block * par_rows
        return (local[None, :] == jnp.arange(par_rows, dtype=jnp.int32)[:, None]).astype(BF16)

    parts = {0: update_for(0)}
    for bits in (3, 2, 1):
        parts[bits] = xor_permute(update_for(bits), "front", bits)
    assembled = jnp.zeros((par_rows, par_rows), F32)
    for bits in range(4):
        which = child_id ^ bits
        moved = jnp.dot(hot(which, pair_id), parts[bits], preferred_element_type=F32)
        assembled = assembled + lax.dot_general(
            moved.astype(BF16),
            hot(which, sibling),
            (((1,), (1,)), ((), ())),
            preferred_element_type=F32,
        )
    return (factor[None, :, :], assembled[:, None, :])


def solution(mesh):
    in_specs = (P("front", "pair", None), P("front", "pair", None), P("front", "pair", None), P())
    out_specs = (P("front", "pair", None), P("pair", "front", None))
    return jax.shard_map(body, mesh=mesh, in_specs=in_specs, out_specs=out_specs, check_vma=False)
```

```python
import functools

import jax
import jax.numpy as jnp
from jax import lax
from jax.experimental import pallas as pl
from jax.experimental.pallas import tpu as pltpu
from jax.sharding import PartitionSpec as P

PO = 3072
LEAF = 128
F32 = jnp.float32
BF16 = jnp.bfloat16


def xor_permute(value, axis, bits):
    return lax.ppermute(value, axis, [(i, i ^ bits) for i in range(lax.axis_size(axis))])


def gather_pair(block):
    far = xor_permute(block, "pair", 2)
    near = xor_permute(block, "pair", 1)
    cross = xor_permute(far, "pair", 1)
    return block, near, far, cross


def halves(value):
    high = value.astype(BF16)
    return high, (value - high.astype(F32)).astype(BF16)


def lane_wide(value, lane):
    lanes = jnp.full((8, LEAF), lane, jnp.int32)
    return jnp.take_along_axis(value, lanes, axis=1, mode="promise_in_bounds")


def columns(groups, lane0):
    return [[lane_wide(group[0], lane0 + k) for k in range(8)] for group in groups]


def row_wide(value, row):
    return jnp.broadcast_to(value[row : row + 1, :], (8, LEAF))


def eliminate(groups, here, after, sub):
    diag, unit = groups[0]
    rest = list(groups[1:])
    cols, below = here[0], here[1:]
    scale = None
    for k in range(8):
        pivot = row_wide(cols[k], k)
        inverse = 1.0 / pivot
        root = lax.rsqrt(pivot)
        scale = root if scale is None else jnp.where(sub == k, root, scale)
        diag_row, unit_row = row_wide(diag, k), row_wide(unit, k)
        factor = jnp.where(sub > k, cols[k] * inverse, 0.0)
        others = [one[k] * inverse for one in below]
        for m in range(k + 1, 8):
            entry = row_wide(cols[m], k)
            cols[m] = cols[m] - factor * entry
            for one, other in zip(below, others):
                one[m] = one[m] - other * entry
        if after:
            for m in range(8):
                entry = row_wide(after[0][m], k)
                for one, other in zip(after, [factor] + others):
                    one[m] = one[m] - other * entry
        diag = diag - factor * diag_row
        unit = unit - factor * unit_row
        rest = [
            (one - other * diag_row, two - other * unit_row)
            for (one, two), other in zip(rest, others)
        ]
    return diag * scale, unit * scale, rest


def factor_leaf(d_ref, x_ref):
    sub = lax.broadcasted_iota(jnp.int32, (8, LEAF), 0)
    x_ref[...] = (
        lax.broadcasted_iota(jnp.int32, (LEAF, LEAF), 0)
        == lax.broadcasted_iota(jnp.int32, (LEAF, LEAF), 1)
    ).astype(F32)
    for start in range(0, LEAF, 32):
        groups = [
            (d_ref[start + g : start + g + 8, :], x_ref[start + g : start + g + 8, :])
            for g in range(0, 32, 8)
        ]
        uppers, inverses = [], []
        here = columns(groups, start)
        for g in range(0, 32, 8):
            after = columns(groups, start + g + 8) if g < 24 else []
            upper, inverse, groups = eliminate(groups, here, after, sub)
            here = after[1:]
            uppers.append(upper)
            inverses.append(inverse)
        upper, inverse = jnp.concatenate(uppers, 0), jnp.concatenate(inverses, 0)
        x_ref[start : start + 32, :] = inverse
        row = start + 32
        if row < LEAF:
            high, low = halves(upper)
            left = jnp.concatenate([high, high, low], 0)
            right = right_three(jnp.concatenate([upper, inverse], 1))
            change = lax.dot_general(
                left, right, (((0,), (0,)), ((), ())), preferred_element_type=F32
            )
            d_ref[row:, :] = d_ref[row:, :] - change[row:, :LEAF]
            x_ref[row:, :] = x_ref[row:, :] - change[row:, LEAF:]


def left_three(value):
    high, low = halves(value)
    return jnp.concatenate([high, high, low], 1)


def right_three(value):
    high, low = halves(value)
    return jnp.concatenate([high, low, high], 0)


def mxu(left, right):
    return jnp.dot(left, right, preferred_element_type=F32)


def factor_kernel(p0, p1, p2, p3, c_ref, f_ref, h_ref, a_ref, w_ref, d_ref, x_ref, l_ref, r_ref):
    pair_id = lax.axis_index("pair")
    rows = p0.shape[0]
    blocks = p0.shape[1] // LEAF
    for bits, part in enumerate((p0, p1, p2, p3)):
        at = pl.multiple_of((pair_id ^ bits) * rows, 64)
        for j in range(blocks):
            a_ref[j, pl.ds(at, rows), :] = part[:, j * LEAF : (j + 1) * LEAF]
    for j in range(blocks):
        w_ref[j] = c_ref[:, j * LEAF : (j + 1) * LEAF]

    def step(k, _):
        here = pl.ds(pl.multiple_of(k * LEAF, LEAF), LEAF)
        d_ref[...] = a_ref[k, here, :]
        factor_leaf(d_ref, x_ref)
        inverse = x_ref[...]
        spread = left_three(inverse)
        panel = mxu(left_three(w_ref[k]), right_three(inverse.T))
        w_ref[k] = panel
        panel3 = left_three(panel)

        def row(j, _):
            upper = mxu(spread, right_three(a_ref[j, here, :]))
            l_ref[j] = left_three(upper.T)
            r_ref[j] = right_three(upper)
            w_ref[j] = w_ref[j] - mxu(panel3, r_ref[j])
            return 0

        lax.fori_loop(k + 1, blocks, row, 0)

        def trail(i, _):
            there = pl.ds(pl.multiple_of(i * LEAF, LEAF), LEAF)

            def one(j, _):
                a_ref[j, there, :] = a_ref[j, there, :] - mxu(l_ref[i], r_ref[j])
                return 0

            lax.fori_loop(i, blocks, one, 0)
            return 0

        lax.fori_loop(k + 1, blocks, trail, 0)
        return 0

    lax.fori_loop(0, blocks, step, 0)
    for j in range(blocks):
        f_ref[:, j * LEAF : (j + 1) * LEAF] = w_ref[j]
        h_ref[:, j * LEAF : (j + 1) * LEAF] = w_ref[j].astype(BF16)


def factor_panel(parts, coupling):
    upd_rows, piv = coupling.shape
    blocks = piv // LEAF
    return pl.pallas_call(
        factor_kernel,
        out_shape=(
            jax.ShapeDtypeStruct((upd_rows, piv), F32),
            jax.ShapeDtypeStruct((upd_rows, piv), BF16),
        ),
        scratch_shapes=[
            pltpu.VMEM((blocks, piv, LEAF), F32),
            pltpu.VMEM((blocks, upd_rows, LEAF), F32),
            pltpu.VMEM((LEAF, LEAF), F32),
            pltpu.VMEM((LEAF, LEAF), F32),
            pltpu.VMEM((blocks, LEAF, 3 * LEAF), BF16),
            pltpu.VMEM((blocks, 3 * LEAF, LEAF), BF16),
        ],
        compiler_params=pltpu.CompilerParams(vmem_limit_bytes=48 << 20),
    )(*parts, coupling)


def hot_block(map_ref, block, upd_rows):
    low = max(0, (block - 2) * LEAF)
    high = min((block + 1) * LEAF, upd_rows)
    rows = lax.broadcasted_iota(jnp.int32, (LEAF, high - low), 0) + block * LEAF
    return (rows == map_ref[:, low:high]).astype(F32).astype(BF16), low, high


def extend_kernel(first, last, *refs):
    part_ref, row_ref, col_ref = refs[:3]
    refs = refs[3:]
    if not first:
        sum_ref, refs = refs[0], refs[1:]
    if last:
        out_ref, moved_ref, flat_ref, sems = refs
    else:
        out_ref, moved_ref = refs
    upd_rows = part_ref.shape[0]
    blocks = moved_ref.shape[1] // LEAF
    for j in range(blocks):
        hot, low, high = hot_block(col_ref, j, upd_rows)
        moved_ref[:, j * LEAF : (j + 1) * LEAF] = lax.dot_general(
            part_ref[:, low:high], hot, (((1,), (1,)), ((), ())), preferred_element_type=F32
        ).astype(BF16)
    copies = []
    for i in range(blocks):
        rows = slice(i * LEAF, (i + 1) * LEAF)
        hot, low, high = hot_block(row_ref, i, upd_rows)
        value = jnp.dot(hot, moved_ref[low:high, :], preferred_element_type=F32)
        if not first:
            value = value + sum_ref[rows, :]
        if last:
            flat_ref[rows, 0, :] = value
            copy = pltpu.make_async_copy(flat_ref.at[rows], out_ref.at[rows], sems.at[i])
            copy.start()
            copies.append(copy)
        else:
            out_ref[rows, :] = value
    for copy in copies:
        copy.wait()


def extend_add(total, part, row_map, col_map, par_rows, last):
    first = total is None
    upd_rows = part.shape[0]
    scratch = [pltpu.VMEM((upd_rows, par_rows), BF16)]
    shape, out_specs = (par_rows, par_rows), pl.BlockSpec(memory_space=pltpu.VMEM)
    if last:
        shape, out_specs = (par_rows, 1, par_rows), pl.BlockSpec(memory_space=pl.ANY)
        scratch += [
            pltpu.VMEM((par_rows, 1, par_rows), F32),
            pltpu.SemaphoreType.DMA((par_rows // LEAF,)),
        ]
    operands = [part, row_map, col_map] + ([] if first else [total])
    return pl.pallas_call(
        functools.partial(extend_kernel, first, last),
        out_shape=jax.ShapeDtypeStruct(shape, F32),
        in_specs=[pl.BlockSpec(memory_space=pltpu.VMEM)] * len(operands),
        out_specs=out_specs,
        scratch_shapes=scratch,
        input_output_aliases={} if first or last else {3: 0},
        cost_estimate=pl.CostEstimate(
            flops=2 * upd_rows * par_rows * par_rows, bytes_accessed=1 << 20, transcendentals=0
        ),
        compiler_params=pltpu.CompilerParams(vmem_limit_bytes=24 << 20),
    )(*operands)


def body(pivot_block, coupling_rows, trailing_block, index_map):
    child_id = lax.axis_index("front")
    pair_id = lax.axis_index("pair")
    pairs = lax.axis_size("pair")
    sibling = child_id % 4
    upd_rows = coupling_rows.shape[1]
    par_rows = PO // pairs
    factor, panel_half = factor_panel(gather_pair(pivot_block[0]), coupling_rows[0])
    panels = gather_pair(panel_half)

    def update_for(bits):
        column = sibling ^ bits
        panel = lax.select_n(column ^ pair_id, *panels)
        product = lax.dot_general(
            panel_half, panel, (((1,), (1,)), ((), ())), preferred_element_type=F32
        )
        trailing = lax.dynamic_slice_in_dim(trailing_block[0], column * upd_rows, upd_rows, 1)
        return (trailing - product).astype(BF16)

    def local_map(which, block):
        own = lax.dynamic_slice(index_map, (which, block * upd_rows), (1, upd_rows))
        return own - block * par_rows

    parts = {}
    for bits in (1, 3, 2):
        parts[bits] = xor_permute(update_for(bits), "front", bits)
    parts[0] = update_for(0)
    assembled = None
    for bits in (0, 1, 3, 2):
        which = child_id ^ bits
        assembled = extend_add(
            assembled,
            parts[bits],
            local_map(which, pair_id),
            local_map(which, sibling),
            par_rows,
            bits == 2,
        )
    return (factor[None, :, :], assembled)


def solution(mesh):
    in_specs = (P("front", "pair", None), P("front", "pair", None), P("front", "pair", None), P())
    out_specs = (P("front", "pair", None), P("pair", "front", None))
    return jax.shard_map(body, mesh=mesh, in_specs=in_specs, out_specs=out_specs, check_vma=False)
```

```python
import functools

import jax
import jax.numpy as jnp
from jax import lax
from jax.experimental import pallas as pl
from jax.experimental.pallas import tpu as pltpu
from jax.sharding import PartitionSpec as P


PO = 3072
LEAF = 128
F32 = jnp.float32
BF16 = jnp.bfloat16


def xor_permute(value, axis, bits):
    return lax.ppermute(value, axis, [(i, i ^ bits) for i in range(lax.axis_size(axis))])


def gather_pair(block):
    far = xor_permute(block, "pair", 2)
    near = xor_permute(block, "pair", 1)
    cross = xor_permute(far, "pair", 1)
    return block, near, far, cross


def gather_pivot(block, pair_id):
    half = block.shape[1] // 2
    quadrant = lax.dynamic_slice_in_dim(block, pair_id // 2 * half, half, 1)
    far = xor_permute(quadrant, "pair", 2)
    near = xor_permute(block, "pair", 1)
    cross = xor_permute(far, "pair", 1)
    return block, near, far, cross


def halves(value):
    high = value.astype(BF16)
    return high, (value - high.astype(F32)).astype(BF16)


def in_hbm(value):
    return pltpu.with_memory_space_constraint(value, pltpu.MemorySpace.HBM)


VMEM = pl.BlockSpec(memory_space=pltpu.VMEM)
HBM = pl.BlockSpec(memory_space=pltpu.MemorySpace.HBM)


def lane_wide(value, lane):
    lanes = jnp.full((8, LEAF), lane, jnp.int32)
    return jnp.take_along_axis(value, lanes, axis=1, mode="promise_in_bounds")


def columns(groups, lane0):
    return [[lane_wide(group[0], lane0 + k) for k in range(8)] for group in groups]


def row_wide(value, row):
    return jnp.broadcast_to(value[row : row + 1, :], (8, LEAF))


def eliminate(groups, here, after, sub):
    diag, unit = groups[0]
    rest = list(groups[1:])
    cols, below = here[0], here[1:]
    scale = None
    for k in range(8):
        pivot = row_wide(cols[k], k)
        inverse = 1.0 / pivot
        root = lax.rsqrt(pivot)
        scale = root if scale is None else jnp.where(sub == k, root, scale)
        diag_row, unit_row = row_wide(diag, k), row_wide(unit, k)
        factor = jnp.where(sub > k, cols[k] * inverse, 0.0)
        others = [one[k] * inverse for one in below]
        for m in range(k + 1, 8):
            entry = row_wide(cols[m], k)
            cols[m] = cols[m] - factor * entry
            for one, other in zip(below, others):
                one[m] = one[m] - other * entry
        if after:
            for m in range(8):
                entry = row_wide(after[0][m], k)
                for one, other in zip(after, [factor] + others):
                    one[m] = one[m] - other * entry
        diag = diag - factor * diag_row
        unit = unit - factor * unit_row
        rest = [
            (one - other * diag_row, two - other * unit_row)
            for (one, two), other in zip(rest, others)
        ]
    return diag * scale, unit * scale, rest


def factor_leaf(d_ref, x_ref):
    sub = lax.broadcasted_iota(jnp.int32, (8, LEAF), 0)
    x_ref[...] = (
        lax.broadcasted_iota(jnp.int32, (LEAF, LEAF), 0)
        == lax.broadcasted_iota(jnp.int32, (LEAF, LEAF), 1)
    ).astype(F32)
    for start in range(0, LEAF, 32):
        groups = [
            (d_ref[start + g : start + g + 8, :], x_ref[start + g : start + g + 8, :])
            for g in range(0, 32, 8)
        ]
        uppers, inverses = [], []
        here = columns(groups, start)
        for g in range(0, 32, 8):
            after = columns(groups[:2], start + g + 8) if g < 24 else []
            upper, inverse, groups = eliminate(groups, here, after, sub)
            here = after[1:] + columns(groups[1:], start + g + 8) if g < 24 else []
            uppers.append(upper)
            inverses.append(inverse)
        upper, inverse = jnp.concatenate(uppers, 0), jnp.concatenate(inverses, 0)
        x_ref[start : start + 32, :] = inverse
        row = start + 32
        if row < LEAF:
            high, low = halves(upper)
            left = jnp.concatenate([high, high, low], 0)
            right = right_three(jnp.concatenate([upper, inverse], 1))
            change = lax.dot_general(
                left, right, (((0,), (0,)), ((), ())), preferred_element_type=F32
            )
            d_ref[row:, :] = d_ref[row:, :] - change[row:, :LEAF]
            x_ref[row:, :] = x_ref[row:, :] - change[row:, LEAF:]


def right_three(value):
    high, low = halves(value)
    return jnp.concatenate([high, low, high], 0)


def three(left, right):
    dot = functools.partial(jnp.dot, preferred_element_type=F32)
    return dot(left[0], right[0]) + (dot(left[0], right[1]) + dot(left[1], right[0]))


def span(first, last):
    return slice(first * LEAF, last * LEAF)


class Columns:
    def __init__(self, pieces, axis):
        self.pieces, self.axis = pieces, axis

    def _where(self, k):
        for leaves, refs in self.pieces:
            if k in leaves:
                return refs, k - leaves[0]

    def get(self, count, other):
        out = []
        for half in range(2):
            parts = []
            for leaves, refs in self.pieces:
                size = min(count, leaves[-1] + 1) - leaves[0]
                if size > 0:
                    at = span(0, size)
                    parts.append(refs[half][(at, other) if self.axis == 0 else (other, at)])
            out.append(jnp.concatenate(parts, self.axis))
        return out

    def put(self, k, other, value):
        refs, slot = self._where(k)
        at = span(slot, slot + 1)
        index = (at, other) if self.axis == 0 else (other, at)
        refs[0][index], refs[1][index] = halves(value)


def stage_kernel(stages, index, blocks, *refs):
    leaves = stages[index]
    keep = leaves[0] + 1 < blocks
    n_out = 7 if keep else 3
    if index == 0:
        own, near, far, cross, c_hbm = refs[:5]
        outs = refs[5 : 5 + n_out + 3]
        d_ref, x_ref, sems = refs[5 + n_out + 3 :]
        a_ref, c_ref, inverse_ref = outs[n_out:]
        pair_id = lax.axis_index("pair")
        rows = own.shape[0]

        def at(bits):
            return pl.ds(pl.multiple_of((pair_id ^ bits) * rows, 64), rows)

        own_copy = pltpu.make_async_copy(own, a_ref.at[at(0)], sems.at[0])
        own_copy.start()
        coupling_copy = pltpu.make_async_copy(c_hbm, c_ref, sems.at[1])
        coupling_copy.start()
        half = blocks // 2
        width = half * LEAF
        there = pl.ds(pl.multiple_of((1 - pair_id // 2) * width, LEAF), width)
        a_ref[at(1), :] = near[...]
        a_ref[at(2), there] = far[...]
        a_ref[at(3), there] = cross[...]
        own_copy.wait()

        @pl.when(pair_id >= 2)
        def _():
            for i in range(half, blocks):
                for j in range(half):
                    low, high = span(i, i + 1), span(j, j + 1)
                    a_ref[high, low] = a_ref[low, high].T

        earlier = []
    else:
        a_ref, c_ref = refs[:2]
        earlier = refs[2 : 2 + 6 * index]
        outs = refs[2 + 6 * index : 2 + 6 * index + n_out]
        d_ref, x_ref = refs[2 + 6 * index + n_out :]
    uppers, lowers, panels = [], [], []
    for i in range(index):
        p_high, p_low, u_high, u_low, l_high, l_low = earlier[6 * i : 6 * i + 6]
        panels.append((stages[i], (p_high, p_low)))
        uppers.append((stages[i], (u_high, u_low)))
        lowers.append((stages[i], (l_high, l_low)))
    panel_ref, p_high, p_low = outs[:3]
    panels.append((leaves, (p_high, p_low)))
    if keep:
        uppers.append((leaves, outs[3:5]))
        lowers.append((leaves, outs[5:7]))
    uppers, lowers, panels = Columns(uppers, 0), Columns(lowers, 1), Columns(panels, 1)
    every = slice(None)
    for slot, k in enumerate(leaves):
        here, rest = span(k, k + 1), span(k + 1, blocks)
        diag = a_ref[here, here]
        if k:
            diag = diag - three(lowers.get(k, here), uppers.get(k, here))
        d_ref[slot] = diag
        side = None
        if k and k + 1 < blocks:
            side = a_ref[here, rest] - three(lowers.get(k, here), uppers.get(k, rest))
        elif k + 1 < blocks:
            side = a_ref[here, rest]
        if k:
            coupled = c_ref[:, here] - three(panels.get(k, every), uppers.get(k, here))
        factor_leaf(d_ref.at[slot], x_ref.at[slot])
        inverse = x_ref[slot]
        if index == 0:
            inverse_ref[slot] = inverse
        if k == 0:
            coupling_copy.wait()
            coupled = c_ref[:, here]
        if side is not None:
            upper = three(halves(inverse), halves(side))
            uppers.put(k, rest, upper)
            for j in range(k + 1, blocks):
                lowers.put(k, span(j, j + 1), upper[:, span(j - k - 1, j - k)].T)
        panel = three(halves(coupled), halves(inverse.T))
        panel_ref[:, span(slot, slot + 1)] = panel
        panels.put(k, every, panel)


def stage(stages, index, blocks, operands, upd_rows, piv):
    width = len(stages[index]) * LEAF
    first, keep = index == 0, stages[index][0] + 1 < blocks
    shapes = [((upd_rows, width), F32)] + [((upd_rows, width), BF16)] * 2
    if keep:
        shapes += [((width, piv), BF16)] * 2 + [((piv, width), BF16)] * 2
    scratch = [pltpu.VMEM((len(stages[index]), LEAF, LEAF), F32)] * 2
    in_specs = [VMEM] * len(operands)
    if first:
        shapes += [((piv, piv), F32), ((upd_rows, piv), F32)]
        shapes += [((len(stages[0]), LEAF, LEAF), F32)]
        scratch.append(pltpu.SemaphoreType.DMA((2,)))
        in_specs = [HBM, VMEM, VMEM, VMEM, HBM]
        operands = [in_hbm(operands[0]), *operands[1:4], in_hbm(operands[4])]
    return pl.pallas_call(
        functools.partial(stage_kernel, stages, index, blocks),
        out_shape=[jax.ShapeDtypeStruct(*shape) for shape in shapes],
        in_specs=in_specs,
        out_specs=[VMEM] * len(shapes),
        scratch_shapes=scratch,
        cost_estimate=pl.CostEstimate(
            flops=len(stages[index]) * 2000000000, bytes_accessed=1 << 20, transcendentals=0
        ),
        compiler_params=pltpu.CompilerParams(vmem_limit_bytes=20 << 20),
    )(*operands)


def run_stages(parts, coupling, after_stage):
    upd_rows, piv = coupling.shape
    blocks = piv // LEAF
    columns, operands, base, earlier = [], [*parts, coupling], None, []
    for index in range(len(STAGES)):
        outs = stage(STAGES, index, blocks, operands, upd_rows, piv)
        columns.append(outs[0])
        after_stage(index, outs)
        if index == 0:
            base = outs[7:9]
        earlier += outs[1:7]
        operands = [*base, *earlier]
    return columns


STAGES = ((0, 1), (2, 3), (4, 5))


LATE = 1


def place_panels(sources, all_ref, at):
    pair_id = lax.axis_index("pair")
    width = sources[0].shape[1]
    for bits, source in enumerate(sources):
        all_ref[pair_id ^ bits, :, at : at + width] = source[...]


def gram(left, right):
    return lax.dot_general(left, right, (((1,), (1,)), ((), ())), preferred_element_type=F32)


def partial_kernel(own_block, *refs):
    t_ref, own_ref, near, far, cross, inverse_ref, u_high, u_low, *sources, w_ref, all_ref = refs
    pair_id = lax.axis_index("pair")
    width = own_ref.shape[1]
    all_ref[pair_id, :, :width] = own_ref[...]
    first, second = inverse_ref[0].T, inverse_ref[1].T
    at = span(0, 1), span(1, 2)
    corner = three(halves(three(halves(first), (u_high[at], u_low[at]))), halves(second))
    whole = jnp.concatenate([first, -corner], 1), jnp.concatenate([0.0 * second, second], 1)
    whole = halves(jnp.concatenate(whole, 0))
    tile = own_ref.shape[0] // 4

    def panel_rows(i, _):
        rows = pl.ds(pl.multiple_of(i * tile, 16), tile)
        for bits, early in ((1, near), (2, far), (3, cross)):
            panel = three(halves(early[rows, :]), whole)
            all_ref[pair_id ^ bits, rows, :width] = panel.astype(BF16)
        return 0

    lax.fori_loop(0, 4, panel_rows, 0)
    at = width
    for chunk in range(len(sources) // 4):
        four = sources[4 * chunk : 4 * chunk + 4]
        place_panels(four, all_ref, at)
        at += four[0].shape[1]
    sibling = lax.rem(lax.axis_index("front"), 4)
    upd_rows = t_ref.shape[0]

    def rows_of(i, _):
        rows = pl.ds(pl.multiple_of(i * tile, 16), tile)
        own = [own_ref[rows, :]] + [sources[i][rows, :] for i in range(0, len(sources), 4)]
        own = jnp.concatenate(own, 1)
        for column in range(4):

            @pl.when((sibling == column) == own_block)
            def _():
                trailing = t_ref[rows, column * upd_rows : (column + 1) * upd_rows]
                w_ref[sibling ^ column, rows, :] = trailing - gram(own, all_ref[column])

        return 0

    lax.fori_loop(0, 4, rows_of, 0)


def partial_update(trailing, first, early, chunks, own_block):
    upd_rows = trailing.shape[0]
    width = first[1].shape[1] + sum(chunk[0].shape[1] for chunk in chunks)
    start = [trailing, first[1], *early[1:], first[9], first[3], first[4]]
    sources = [source for chunk in chunks for source in chunk]
    return pl.pallas_call(
        functools.partial(partial_kernel, own_block),
        out_shape=jax.ShapeDtypeStruct((4, upd_rows, upd_rows), F32),
        in_specs=[VMEM] * (len(start) + len(sources)),
        out_specs=VMEM,
        scratch_shapes=[pltpu.VMEM((4, upd_rows, width), BF16)],
        cost_estimate=pl.CostEstimate(flops=8000000000, bytes_accessed=1 << 20, transcendentals=0),
        compiler_params=pltpu.CompilerParams(vmem_limit_bytes=24 << 20),
    )(*start, *sources)


def finish_kernel(bits, n_sources, w_ref, *refs):
    sources, refs = refs[:n_sources], refs[n_sources:]
    copies = []
    if bits == 0:
        columns, (u_ref, f_ref, all_ref, sems) = refs[:-4], refs[-4:]
        at = 0
        for i, column in enumerate(columns):
            width = column.shape[1]
            copies.append(pltpu.make_async_copy(column, f_ref.at[:, at : at + width], sems.at[i]))
            copies[-1].start()
            at += width
    else:
        u_ref, all_ref = refs
    at = 0
    for first in range(0, n_sources, 4):
        place_panels(sources[first : first + 4], all_ref, at)
        at += sources[first].shape[1]
    own = jnp.concatenate([sources[i][...] for i in range(0, n_sources, 4)], 1)
    sibling = lax.rem(lax.axis_index("front"), 4)
    u_ref[...] = (w_ref[bits] - gram(own, all_ref[sibling ^ bits])).astype(BF16)
    for copy in copies:
        copy.wait()


def finish_update(partial, chunks, bits, columns=()):
    upd_rows = partial.shape[1]
    sources = [source for chunk in chunks for source in chunk]
    width = sum(chunk[0].shape[1] for chunk in chunks)
    shapes = [jax.ShapeDtypeStruct((upd_rows, upd_rows), BF16)]
    out_specs = [VMEM]
    scratch = [pltpu.VMEM((4, upd_rows, width), BF16)]
    if columns:
        piv = sum(column.shape[1] for column in columns)
        shapes.append(jax.ShapeDtypeStruct((upd_rows, piv), F32))
        out_specs.append(HBM)
        scratch.append(pltpu.SemaphoreType.DMA((len(columns),)))
    return pl.pallas_call(
        functools.partial(finish_kernel, bits, len(sources)),
        out_shape=shapes,
        in_specs=[VMEM] * (1 + len(sources) + len(columns)),
        out_specs=out_specs,
        scratch_shapes=scratch,
        cost_estimate=pl.CostEstimate(flops=500000000, bytes_accessed=1 << 20, transcendentals=0),
        compiler_params=pltpu.CompilerParams(vmem_limit_bytes=12 << 20),
    )(partial, *sources, *columns)


def hot_block(map_ref, block, upd_rows):
    low = max(0, (block - 2) * LEAF)
    high = min((block + 1) * LEAF, upd_rows)
    rows = lax.broadcasted_iota(jnp.int32, (LEAF, high - low), 0) + block * LEAF
    return (rows == map_ref[:, low:high]).astype(F32).astype(BF16), low, high


def extend_kernel(first, last, *refs):
    part_ref, row_ref, col_ref = refs[:3]
    refs = refs[3:]
    if not first:
        sum_ref, refs = refs[0], refs[1:]
    if last:
        out_ref, moved_ref, flat_ref, sems = refs
    else:
        out_ref, moved_ref = refs
    upd_rows = part_ref.shape[0]
    blocks = moved_ref.shape[1] // LEAF
    for j in range(blocks):
        hot, low, high = hot_block(col_ref, j, upd_rows)
        moved_ref[:, j * LEAF : (j + 1) * LEAF] = lax.dot_general(
            part_ref[:, low:high], hot, (((1,), (1,)), ((), ())), preferred_element_type=F32
        ).astype(BF16)
    copies = []
    for i in range(blocks):
        rows = slice(i * LEAF, (i + 1) * LEAF)
        hot, low, high = hot_block(row_ref, i, upd_rows)
        value = jnp.dot(hot, moved_ref[low:high, :], preferred_element_type=F32)
        if not first:
            value = value + sum_ref[rows, :]
        if last:
            flat_ref[rows, 0, :] = value
            copy = pltpu.make_async_copy(flat_ref.at[rows], out_ref.at[rows], sems.at[i])
            copy.start()
            copies.append(copy)
        else:
            out_ref[rows, :] = value
    for copy in copies:
        copy.wait()


def extend_add(total, part, row_map, col_map, par_rows, last):
    first = total is None
    upd_rows = part.shape[0]
    scratch = [pltpu.VMEM((upd_rows, par_rows), BF16)]
    shape, out_specs = (par_rows, par_rows), pl.BlockSpec(memory_space=pltpu.VMEM)
    if last:
        shape, out_specs = (par_rows, 1, par_rows), HBM
        scratch += [
            pltpu.VMEM((par_rows, 1, par_rows), F32),
            pltpu.SemaphoreType.DMA((par_rows // LEAF,)),
        ]
    operands = [part, row_map, col_map] + ([] if first else [total])
    return pl.pallas_call(
        functools.partial(extend_kernel, first, last),
        out_shape=jax.ShapeDtypeStruct(shape, F32),
        in_specs=[pl.BlockSpec(memory_space=pltpu.VMEM)] * len(operands),
        out_specs=out_specs,
        scratch_shapes=scratch,
        input_output_aliases={} if first or last else {3: 0},
        cost_estimate=pl.CostEstimate(
            flops=2 * upd_rows * par_rows * par_rows, bytes_accessed=1 << 20, transcendentals=0
        ),
        compiler_params=pltpu.CompilerParams(vmem_limit_bytes=24 << 20),
    )(*operands)


def level(pivot_block, coupling_rows, trailing_block, index_map):
    child_id = lax.axis_index("front")
    pair_id = lax.axis_index("pair")
    pairs = lax.axis_size("pair")
    sibling = child_id % 4
    upd_rows = coupling_rows.shape[1]
    par_rows = PO // pairs
    parts = gather_pivot(pivot_block[0], pair_id)
    early = coupling_rows[0, :, : len(STAGES[0]) * LEAF]
    early = gather_pair(early)
    chunks, firsts = [], []

    def after_stage(index, outs):
        if index == 0:
            firsts.append(outs)
        else:
            chunks.append(gather_pair(outs[1]))

    columns = run_stages(parts, coupling_rows[0], after_stage)
    partial = partial_update(trailing_block[0], firsts[0], early, chunks[:-LATE], False)

    def local_map(which, block):
        own = lax.dynamic_slice(index_map, (which, block * upd_rows), (1, upd_rows))
        return own - block * par_rows

    maps = [
        (local_map(child_id ^ bits, pair_id), local_map(child_id ^ bits, sibling))
        for bits in range(4)
    ]
    parts = {}
    for bits in (3, 1, 2):
        (update,) = finish_update(partial, chunks[-LATE:], bits)
        parts[bits] = xor_permute(update, "front", bits)
    owned = partial_update(trailing_block[0], firsts[0], early, chunks[:-LATE], True)
    parts[0], factor = finish_update(owned, chunks[-LATE:], 0, columns)
    assembled = None
    for bits in (0, 3, 1, 2):
        assembled = extend_add(assembled, parts[bits], *maps[bits], par_rows, bits == 2)
    return (factor[None, :, :], assembled)


def solution(mesh):
    in_specs = (P("front", "pair", None), P("front", "pair", None), P("front", "pair", None), P())
    out_specs = (P("front", "pair", None), P("pair", "front", None))
    return jax.shard_map(level, mesh=mesh, in_specs=in_specs, out_specs=out_specs, check_vma=False)
```

```python
import functools

import jax
import jax.numpy as jnp
from jax import lax
from jax.experimental import pallas as pl
from jax.experimental.pallas import tpu as pltpu
from jax.sharding import PartitionSpec as P


PO = 3072
LEAF = 128
F32 = jnp.float32
BF16 = jnp.bfloat16


def xor_permute(value, axis, bits):
    return lax.ppermute(value, axis, [(i, i ^ bits) for i in range(lax.axis_size(axis))])


def gather_pair(block):
    far = xor_permute(block, "pair", 2)
    near = xor_permute(block, "pair", 1)
    cross = xor_permute(far, "pair", 1)
    return block, near, far, cross


def gather_pivot(block, pair_id):
    half = block.shape[1] // 2
    quadrant = lax.dynamic_slice_in_dim(block, pair_id // 2 * half, half, 1)
    far = xor_permute(quadrant, "pair", 2)
    near = xor_permute(block, "pair", 1)
    cross = xor_permute(far, "pair", 1)
    return block, near, far, cross


def halves(value):
    high = value.astype(BF16)
    return high, (value - high.astype(F32)).astype(BF16)


def in_hbm(value):
    return pltpu.with_memory_space_constraint(value, pltpu.MemorySpace.HBM)


VMEM = pl.BlockSpec(memory_space=pltpu.VMEM)
HBM = pl.BlockSpec(memory_space=pltpu.MemorySpace.HBM)


def lane_wide(value, lane):
    lanes = jnp.full((8, LEAF), lane, jnp.int32)
    return jnp.take_along_axis(value, lanes, axis=1, mode="promise_in_bounds")


def columns(groups, lane0):
    return [[lane_wide(group[0], lane0 + k) for k in range(8)] for group in groups]


def row_wide(value, row):
    return jnp.broadcast_to(value[row : row + 1, :], (8, LEAF))


def eliminate(groups, here, after, sub):
    diag, unit = groups[0]
    rest = list(groups[1:])
    cols, below = here[0], here[1:]
    scale = None
    for k in range(8):
        pivot = row_wide(cols[k], k)
        inverse = 1.0 / pivot
        root = lax.rsqrt(pivot)
        scale = root if scale is None else jnp.where(sub == k, root, scale)
        diag_row, unit_row = row_wide(diag, k), row_wide(unit, k)
        factor = jnp.where(sub > k, cols[k] * inverse, 0.0)
        others = [one[k] * inverse for one in below]
        for m in range(k + 1, 8):
            entry = row_wide(cols[m], k)
            cols[m] = cols[m] - factor * entry
            for one, other in zip(below, others):
                one[m] = one[m] - other * entry
        if after:
            for m in range(8):
                entry = row_wide(after[0][m], k)
                for one, other in zip(after, [factor] + others):
                    one[m] = one[m] - other * entry
        diag = diag - factor * diag_row
        unit = unit - factor * unit_row
        rest = [
            (one - other * diag_row, two - other * unit_row)
            for (one, two), other in zip(rest, others)
        ]
    return diag * scale, unit * scale, rest


def factor_leaf(d_ref, x_ref):
    sub = lax.broadcasted_iota(jnp.int32, (8, LEAF), 0)
    x_ref[...] = (
        lax.broadcasted_iota(jnp.int32, (LEAF, LEAF), 0)
        == lax.broadcasted_iota(jnp.int32, (LEAF, LEAF), 1)
    ).astype(F32)
    for start in range(0, LEAF, 32):
        groups = [
            (d_ref[start + g : start + g + 8, :], x_ref[start + g : start + g + 8, :])
            for g in range(0, 32, 8)
        ]
        uppers, inverses = [], []
        here = columns(groups, start)
        for g in range(0, 32, 8):
            after = columns(groups[:2], start + g + 8) if g < 24 else []
            upper, inverse, groups = eliminate(groups, here, after, sub)
            here = after[1:] + columns(groups[1:], start + g + 8) if g < 24 else []
            uppers.append(upper)
            inverses.append(inverse)
        upper, inverse = jnp.concatenate(uppers, 0), jnp.concatenate(inverses, 0)
        x_ref[start : start + 32, :] = inverse
        row = start + 32
        if row < LEAF:
            high, low = halves(upper)
            left = jnp.concatenate([high, high, low], 0)
            right = right_three(jnp.concatenate([upper, inverse], 1))
            change = lax.dot_general(
                left, right, (((0,), (0,)), ((), ())), preferred_element_type=F32
            )
            d_ref[row:, :] = d_ref[row:, :] - change[row:, :LEAF]
            x_ref[row:, :] = x_ref[row:, :] - change[row:, LEAF:]


def right_three(value):
    high, low = halves(value)
    return jnp.concatenate([high, low, high], 0)


def three(left, right):
    dot = functools.partial(jnp.dot, preferred_element_type=F32)
    return dot(left[0], right[0]) + (dot(left[0], right[1]) + dot(left[1], right[0]))


def span(first, last):
    return slice(first * LEAF, last * LEAF)


class Columns:
    def __init__(self, pieces, axis):
        self.pieces, self.axis = pieces, axis

    def _where(self, k):
        for leaves, refs in self.pieces:
            if k in leaves:
                return refs, k - leaves[0]

    def get(self, count, other):
        out = []
        for half in range(2):
            parts = []
            for leaves, refs in self.pieces:
                size = min(count, leaves[-1] + 1) - leaves[0]
                if size > 0:
                    at = span(0, size)
                    parts.append(refs[half][(at, other) if self.axis == 0 else (other, at)])
            out.append(jnp.concatenate(parts, self.axis))
        return out

    def put(self, k, other, value):
        refs, slot = self._where(k)
        at = span(slot, slot + 1)
        index = (at, other) if self.axis == 0 else (other, at)
        refs[0][index], refs[1][index] = halves(value)


def stage_kernel(stages, index, blocks, *refs):
    leaves = stages[index]
    keep = leaves[0] + 1 < blocks
    n_out = 7 if keep else 3
    if index == 0:
        own, near, far, cross, c_hbm = refs[:5]
        outs = refs[5 : 5 + n_out + 3]
        d_ref, x_ref, sems = refs[5 + n_out + 3 :]
        a_ref, c_ref, inverse_ref = outs[n_out:]
        pair_id = lax.axis_index("pair")
        rows = own.shape[0]

        def at(bits):
            return pl.ds(pl.multiple_of((pair_id ^ bits) * rows, 64), rows)

        own_copy = pltpu.make_async_copy(own, a_ref.at[at(0)], sems.at[0])
        own_copy.start()
        coupling_copy = pltpu.make_async_copy(c_hbm, c_ref, sems.at[1])
        coupling_copy.start()
        half = blocks // 2
        width = half * LEAF
        there = pl.ds(pl.multiple_of((1 - pair_id // 2) * width, LEAF), width)
        a_ref[at(1), :] = near[...]
        a_ref[at(2), there] = far[...]
        a_ref[at(3), there] = cross[...]
        own_copy.wait()

        @pl.when(pair_id >= 2)
        def _():
            for i in range(half, blocks):
                for j in range(half):
                    low, high = span(i, i + 1), span(j, j + 1)
                    a_ref[high, low] = a_ref[low, high].T

        earlier = []
    else:
        a_ref, c_ref = refs[:2]
        earlier = refs[2 : 2 + 6 * index]
        outs = refs[2 + 6 * index : 2 + 6 * index + n_out]
        d_ref, x_ref = refs[2 + 6 * index + n_out :]
    uppers, lowers, panels = [], [], []
    for i in range(index):
        p_high, p_low, u_high, u_low, l_high, l_low = earlier[6 * i : 6 * i + 6]
        panels.append((stages[i], (p_high, p_low)))
        uppers.append((stages[i], (u_high, u_low)))
        lowers.append((stages[i], (l_high, l_low)))
    panel_ref, p_high, p_low = outs[:3]
    panels.append((leaves, (p_high, p_low)))
    if keep:
        uppers.append((leaves, outs[3:5]))
        lowers.append((leaves, outs[5:7]))
    uppers, lowers, panels = Columns(uppers, 0), Columns(lowers, 1), Columns(panels, 1)
    every = slice(None)
    for slot, k in enumerate(leaves):
        here, rest = span(k, k + 1), span(k + 1, blocks)
        diag = a_ref[here, here]
        if k:
            diag = diag - three(lowers.get(k, here), uppers.get(k, here))
        d_ref[slot] = diag
        side = None
        if k and k + 1 < blocks:
            side = a_ref[here, rest] - three(lowers.get(k, here), uppers.get(k, rest))
        elif k + 1 < blocks:
            side = a_ref[here, rest]
        if k:
            coupled = c_ref[:, here] - three(panels.get(k, every), uppers.get(k, here))
        factor_leaf(d_ref.at[slot], x_ref.at[slot])
        inverse = x_ref[slot]
        if index == 0:
            inverse_ref[slot] = inverse
        if k == 0:
            coupling_copy.wait()
            coupled = c_ref[:, here]
        if side is not None:
            upper = three(halves(inverse), halves(side))
            uppers.put(k, rest, upper)
            for j in range(k + 1, blocks):
                lowers.put(k, span(j, j + 1), upper[:, span(j - k - 1, j - k)].T)
        panel = three(halves(coupled), halves(inverse.T))
        panel_ref[:, span(slot, slot + 1)] = panel
        panels.put(k, every, panel)


def stage(stages, index, blocks, operands, upd_rows, piv):
    width = len(stages[index]) * LEAF
    first, keep = index == 0, stages[index][0] + 1 < blocks
    shapes = [((upd_rows, width), F32)] + [((upd_rows, width), BF16)] * 2
    if keep:
        shapes += [((width, piv), BF16)] * 2 + [((piv, width), BF16)] * 2
    scratch = [pltpu.VMEM((len(stages[index]), LEAF, LEAF), F32)] * 2
    in_specs = [VMEM] * len(operands)
    if first:
        shapes += [((piv, piv), F32), ((upd_rows, piv), F32)]
        shapes += [((len(stages[0]), LEAF, LEAF), F32)]
        scratch.append(pltpu.SemaphoreType.DMA((2,)))
        in_specs = [HBM, VMEM, VMEM, VMEM, HBM]
        operands = [in_hbm(operands[0]), *operands[1:4], in_hbm(operands[4])]
    return pl.pallas_call(
        functools.partial(stage_kernel, stages, index, blocks),
        out_shape=[jax.ShapeDtypeStruct(*shape) for shape in shapes],
        in_specs=in_specs,
        out_specs=[VMEM] * len(shapes),
        scratch_shapes=scratch,
        cost_estimate=pl.CostEstimate(
            flops=len(stages[index]) * 2000000000, bytes_accessed=1 << 20, transcendentals=0
        ),
        compiler_params=pltpu.CompilerParams(vmem_limit_bytes=20 << 20),
    )(*operands)


def run_stages(parts, coupling, after_stage):
    upd_rows, piv = coupling.shape
    blocks = piv // LEAF
    columns, operands, base, earlier = [], [*parts, coupling], None, []
    for index in range(len(STAGES)):
        outs = stage(STAGES, index, blocks, operands, upd_rows, piv)
        columns.append(outs[0])
        after_stage(index, outs)
        if index == 0:
            base = outs[7:9]
        earlier += outs[1:7]
        operands = [*base, *earlier]
    return columns


STAGES = ((0, 1), (2, 3), (4, 5))


LATE = 1
FIRST = 3


def place_panels(sources, all_ref, at):
    pair_id = lax.axis_index("pair")
    width = sources[0].shape[1]
    for bits, source in enumerate(sources):
        all_ref[pair_id ^ bits, :, at : at + width] = source[...]


def gram(left, right):
    return lax.dot_general(left, right, (((1,), (1,)), ((), ())), preferred_element_type=F32)


def partial_kernel(ahead, *refs):
    t_ref, own_ref, near, far, cross, inverse_ref, u_high, u_low, *sources, w_ref, all_ref = refs
    pair_id = lax.axis_index("pair")
    width = own_ref.shape[1]
    all_ref[pair_id, :, :width] = own_ref[...]
    first, second = inverse_ref[0].T, inverse_ref[1].T
    at = span(0, 1), span(1, 2)
    corner = three(halves(three(halves(first), (u_high[at], u_low[at]))), halves(second))
    whole = jnp.concatenate([first, -corner], 1), jnp.concatenate([0.0 * second, second], 1)
    whole = halves(jnp.concatenate(whole, 0))
    tile = own_ref.shape[0] // 4

    def panel_rows(i, _):
        rows = pl.ds(pl.multiple_of(i * tile, 16), tile)
        for bits, early in ((1, near), (2, far), (3, cross)):
            panel = three(halves(early[rows, :]), whole)
            all_ref[pair_id ^ bits, rows, :width] = panel.astype(BF16)
        return 0

    lax.fori_loop(0, 4, panel_rows, 0)
    at = width
    for chunk in range(len(sources) // 4):
        four = sources[4 * chunk : 4 * chunk + 4]
        place_panels(four, all_ref, at)
        at += four[0].shape[1]
    sibling = lax.rem(lax.axis_index("front"), 4)
    upd_rows = t_ref.shape[0]

    def rows_of(i, _):
        rows = pl.ds(pl.multiple_of(i * tile, 16), tile)
        own = [own_ref[rows, :]] + [sources[i][rows, :] for i in range(0, len(sources), 4)]
        own = jnp.concatenate(own, 1)
        for column in range(4):

            @pl.when((sibling == column ^ FIRST) == ahead)
            def _():
                trailing = t_ref[rows, column * upd_rows : (column + 1) * upd_rows]
                w_ref[sibling ^ column, rows, :] = trailing - gram(own, all_ref[column])

        return 0

    lax.fori_loop(0, 4, rows_of, 0)


def partial_update(trailing, first, early, chunks, ahead):
    upd_rows = trailing.shape[0]
    width = first[1].shape[1] + sum(chunk[0].shape[1] for chunk in chunks)
    start = [trailing, first[1], *early[1:], first[9], first[3], first[4]]
    sources = [source for chunk in chunks for source in chunk]
    return pl.pallas_call(
        functools.partial(partial_kernel, ahead),
        out_shape=jax.ShapeDtypeStruct((4, upd_rows, upd_rows), F32),
        in_specs=[VMEM] * (len(start) + len(sources)),
        out_specs=VMEM,
        scratch_shapes=[pltpu.VMEM((4, upd_rows, width), BF16)],
        cost_estimate=pl.CostEstimate(flops=8000000000, bytes_accessed=1 << 20, transcendentals=0),
        compiler_params=pltpu.CompilerParams(vmem_limit_bytes=24 << 20),
    )(*start, *sources)


def finish_kernel(bits, n_sources, w_ref, *refs):
    sources, refs = refs[:n_sources], refs[n_sources:]
    copies = []
    if bits == 0:
        columns, (u_ref, f_ref, all_ref, sems) = refs[:-4], refs[-4:]
        at = 0
        for i, column in enumerate(columns):
            width = column.shape[1]
            copies.append(pltpu.make_async_copy(column, f_ref.at[:, at : at + width], sems.at[i]))
            copies[-1].start()
            at += width
    else:
        u_ref, all_ref = refs
    at = 0
    for first in range(0, n_sources, 4):
        place_panels(sources[first : first + 4], all_ref, at)
        at += sources[first].shape[1]
    own = jnp.concatenate([sources[i][...] for i in range(0, n_sources, 4)], 1)
    sibling = lax.rem(lax.axis_index("front"), 4)
    u_ref[...] = (w_ref[bits] - gram(own, all_ref[sibling ^ bits])).astype(BF16)
    for copy in copies:
        copy.wait()


def finish_update(partial, chunks, bits, columns=()):
    upd_rows = partial.shape[1]
    sources = [source for chunk in chunks for source in chunk]
    width = sum(chunk[0].shape[1] for chunk in chunks)
    shapes = [jax.ShapeDtypeStruct((upd_rows, upd_rows), BF16)]
    out_specs = [VMEM]
    scratch = [pltpu.VMEM((4, upd_rows, width), BF16)]
    if columns:
        piv = sum(column.shape[1] for column in columns)
        shapes.append(jax.ShapeDtypeStruct((upd_rows, piv), F32))
        out_specs.append(HBM)
        scratch.append(pltpu.SemaphoreType.DMA((len(columns),)))
    return pl.pallas_call(
        functools.partial(finish_kernel, bits, len(sources)),
        out_shape=shapes,
        in_specs=[VMEM] * (1 + len(sources) + len(columns)),
        out_specs=out_specs,
        scratch_shapes=scratch,
        cost_estimate=pl.CostEstimate(flops=500000000, bytes_accessed=1 << 20, transcendentals=0),
        compiler_params=pltpu.CompilerParams(vmem_limit_bytes=12 << 20),
    )(partial, *sources, *columns)


def hot_block(map_ref, block, upd_rows):
    low = max(0, (block - 2) * LEAF)
    high = min((block + 1) * LEAF, upd_rows)
    rows = lax.broadcasted_iota(jnp.int32, (LEAF, high - low), 0) + block * LEAF
    return (rows == map_ref[:, low:high]).astype(F32).astype(BF16), low, high


def extend_kernel(first, last, *refs):
    part_ref, row_ref, col_ref = refs[:3]
    refs = refs[3:]
    if not first:
        sum_ref, refs = refs[0], refs[1:]
    if last:
        out_ref, moved_ref, flat_ref, sems = refs
    else:
        out_ref, moved_ref = refs
    upd_rows = part_ref.shape[0]
    blocks = moved_ref.shape[1] // LEAF
    for j in range(blocks):
        hot, low, high = hot_block(col_ref, j, upd_rows)
        moved_ref[:, j * LEAF : (j + 1) * LEAF] = lax.dot_general(
            part_ref[:, low:high], hot, (((1,), (1,)), ((), ())), preferred_element_type=F32
        ).astype(BF16)
    copies = []
    for i in range(blocks):
        rows = slice(i * LEAF, (i + 1) * LEAF)
        hot, low, high = hot_block(row_ref, i, upd_rows)
        value = jnp.dot(hot, moved_ref[low:high, :], preferred_element_type=F32)
        if not first:
            value = value + sum_ref[rows, :]
        if last:
            flat_ref[rows, 0, :] = value
            copy = pltpu.make_async_copy(flat_ref.at[rows], out_ref.at[rows], sems.at[i])
            copy.start()
            copies.append(copy)
        else:
            out_ref[rows, :] = value
    for copy in copies:
        copy.wait()


def extend_add(total, part, row_map, col_map, par_rows, last):
    first = total is None
    upd_rows = part.shape[0]
    scratch = [pltpu.VMEM((upd_rows, par_rows), BF16)]
    shape, out_specs = (par_rows, par_rows), pl.BlockSpec(memory_space=pltpu.VMEM)
    if last:
        shape, out_specs = (par_rows, 1, par_rows), HBM
        scratch += [
            pltpu.VMEM((par_rows, 1, par_rows), F32),
            pltpu.SemaphoreType.DMA((par_rows // LEAF,)),
        ]
    operands = [part, row_map, col_map] + ([] if first else [total])
    return pl.pallas_call(
        functools.partial(extend_kernel, first, last),
        out_shape=jax.ShapeDtypeStruct(shape, F32),
        in_specs=[pl.BlockSpec(memory_space=pltpu.VMEM)] * len(operands),
        out_specs=out_specs,
        scratch_shapes=scratch,
        input_output_aliases={} if first or last else {3: 0},
        cost_estimate=pl.CostEstimate(
            flops=2 * upd_rows * par_rows * par_rows, bytes_accessed=1 << 20, transcendentals=0
        ),
        compiler_params=pltpu.CompilerParams(vmem_limit_bytes=24 << 20),
    )(*operands)


def level(pivot_block, coupling_rows, trailing_block, index_map):
    child_id = lax.axis_index("front")
    pair_id = lax.axis_index("pair")
    pairs = lax.axis_size("pair")
    sibling = child_id % 4
    upd_rows = coupling_rows.shape[1]
    par_rows = PO // pairs
    parts = gather_pivot(pivot_block[0], pair_id)
    early = coupling_rows[0, :, : len(STAGES[0]) * LEAF]
    early = gather_pair(early)
    chunks, firsts = [], []

    def after_stage(index, outs):
        if index == 0:
            firsts.append(outs)
        else:
            chunks.append(gather_pair(outs[1]))

    columns = run_stages(parts, coupling_rows[0], after_stage)
    ahead = partial_update(trailing_block[0], firsts[0], early, chunks[:-LATE], True)
    others = partial_update(trailing_block[0], firsts[0], early, chunks[:-LATE], False)

    def local_map(which, block):
        own = lax.dynamic_slice(index_map, (which, block * upd_rows), (1, upd_rows))
        return own - block * par_rows

    maps = [
        (local_map(child_id ^ bits, pair_id), local_map(child_id ^ bits, sibling))
        for bits in range(4)
    ]
    parts = {}
    for bits in (FIRST, 1, 2):
        partial = ahead if bits == FIRST else others
        (update,) = finish_update(partial, chunks[-LATE:], bits)
        parts[bits] = xor_permute(update, "front", bits)
    parts[0], factor = finish_update(others, chunks[-LATE:], 0, columns)
    assembled = None
    for bits in (0, 3, 1, 2):
        assembled = extend_add(assembled, parts[bits], *maps[bits], par_rows, bits == 2)
    return (factor[None, :, :], assembled)


def solution(mesh):
    in_specs = (P("front", "pair", None), P("front", "pair", None), P("front", "pair", None), P())
    out_specs = (P("front", "pair", None), P("pair", "front", None))
    return jax.shard_map(level, mesh=mesh, in_specs=in_specs, out_specs=out_specs, check_vma=False)
```

```python
import functools

import jax
import jax.numpy as jnp
from jax import lax
from jax.experimental import pallas as pl
from jax.experimental.pallas import tpu as pltpu
from jax.sharding import PartitionSpec as P


PO = 3072
LEAF = 128
F32 = jnp.float32
BF16 = jnp.bfloat16


def xor_permute(value, axis, bits):
    return lax.ppermute(value, axis, [(i, i ^ bits) for i in range(lax.axis_size(axis))])


def gather_pair(block):
    far = xor_permute(block, "pair", 2)
    near = xor_permute(block, "pair", 1)
    cross = xor_permute(far, "pair", 1)
    return block, near, far, cross


def gather_pivot(block, pair_id):
    half = block.shape[1] // 2
    quadrant = lax.dynamic_slice_in_dim(block, pair_id // 2 * half, half, 1)
    far = xor_permute(quadrant, "pair", 2)
    near = xor_permute(block, "pair", 1)
    cross = xor_permute(far, "pair", 1)
    return block, near, far, cross


def halves(value):
    high = value.astype(BF16)
    return high, (value - high.astype(F32)).astype(BF16)


def in_hbm(value):
    return pltpu.with_memory_space_constraint(value, pltpu.MemorySpace.HBM)


VMEM = pl.BlockSpec(memory_space=pltpu.VMEM)
HBM = pl.BlockSpec(memory_space=pltpu.MemorySpace.HBM)


def lane_wide(value, lane):
    lanes = jnp.full((8, LEAF), lane, jnp.int32)
    return jnp.take_along_axis(value, lanes, axis=1, mode="promise_in_bounds")


def columns(groups, lane0):
    return [[lane_wide(group[0], lane0 + k) for k in range(8)] for group in groups]


def row_wide(value, row):
    return jnp.broadcast_to(value[row : row + 1, :], (8, LEAF))


def eliminate(groups, here, after, sub):
    diag, unit = groups[0]
    rest = list(groups[1:])
    cols, below = here[0], here[1:]
    scale = None
    for k in range(8):
        pivot = row_wide(cols[k], k)
        inverse = 1.0 / pivot
        root = lax.rsqrt(pivot)
        scale = root if scale is None else jnp.where(sub == k, root, scale)
        diag_row, unit_row = row_wide(diag, k), row_wide(unit, k)
        factor = jnp.where(sub > k, cols[k] * inverse, 0.0)
        others = [one[k] * inverse for one in below]
        for m in range(k + 1, 8):
            entry = row_wide(cols[m], k)
            cols[m] = cols[m] - factor * entry
            for one, other in zip(below, others):
                one[m] = one[m] - other * entry
        if after:
            for m in range(8):
                entry = row_wide(after[0][m], k)
                for one, other in zip(after, [factor] + others):
                    one[m] = one[m] - other * entry
        diag = diag - factor * diag_row
        unit = unit - factor * unit_row
        rest = [
            (one - other * diag_row, two - other * unit_row)
            for (one, two), other in zip(rest, others)
        ]
    return diag * scale, unit * scale, rest


def factor_leaf(d_ref, x_ref):
    sub = lax.broadcasted_iota(jnp.int32, (8, LEAF), 0)
    x_ref[...] = (
        lax.broadcasted_iota(jnp.int32, (LEAF, LEAF), 0)
        == lax.broadcasted_iota(jnp.int32, (LEAF, LEAF), 1)
    ).astype(F32)
    for start in range(0, LEAF, 32):
        groups = [
            (d_ref[start + g : start + g + 8, :], x_ref[start + g : start + g + 8, :])
            for g in range(0, 32, 8)
        ]
        uppers, inverses = [], []
        here = columns(groups, start)
        for g in range(0, 32, 8):
            after = columns(groups[:2], start + g + 8) if g < 24 else []
            upper, inverse, groups = eliminate(groups, here, after, sub)
            here = after[1:] + columns(groups[1:], start + g + 8) if g < 24 else []
            uppers.append(upper)
            inverses.append(inverse)
        upper, inverse = jnp.concatenate(uppers, 0), jnp.concatenate(inverses, 0)
        x_ref[start : start + 32, :] = inverse
        row = start + 32
        if row < LEAF:
            high, low = halves(upper)
            left = jnp.concatenate([high, high, low], 0)
            right = right_three(jnp.concatenate([upper, inverse], 1))
            change = lax.dot_general(
                left, right, (((0,), (0,)), ((), ())), preferred_element_type=F32
            )
            d_ref[row:, :] = d_ref[row:, :] - change[row:, :LEAF]
            x_ref[row:, :] = x_ref[row:, :] - change[row:, LEAF:]


def right_three(value):
    high, low = halves(value)
    return jnp.concatenate([high, low, high], 0)


def three(left, right):
    dot = functools.partial(jnp.dot, preferred_element_type=F32)
    return dot(left[0], right[0]) + (dot(left[0], right[1]) + dot(left[1], right[0]))


def span(first, last):
    return slice(first * LEAF, last * LEAF)


class Columns:
    def __init__(self, pieces, axis):
        self.pieces, self.axis = pieces, axis

    def _where(self, k):
        for leaves, refs in self.pieces:
            if k in leaves:
                return refs, k - leaves[0]

    def get(self, count, other):
        out = []
        for half in range(2):
            parts = []
            for leaves, refs in self.pieces:
                size = min(count, leaves[-1] + 1) - leaves[0]
                if size > 0:
                    at = span(0, size)
                    parts.append(refs[half][(at, other) if self.axis == 0 else (other, at)])
            out.append(jnp.concatenate(parts, self.axis))
        return out

    def put(self, k, other, value):
        refs, slot = self._where(k)
        at = span(slot, slot + 1)
        index = (at, other) if self.axis == 0 else (other, at)
        refs[0][index], refs[1][index] = halves(value)


def stage_kernel(stages, index, blocks, *refs):
    leaves = stages[index]
    keep = leaves[0] + 1 < blocks
    n_out = 7 if keep else 3
    if index == 0:
        own, near, far, cross, c_hbm = refs[:5]
        outs = refs[5 : 5 + n_out + 3]
        d_ref, x_ref, sems = refs[5 + n_out + 3 :]
        a_ref, c_ref, inverse_ref = outs[n_out:]
        pair_id = lax.axis_index("pair")
        rows = own.shape[0]

        def at(bits):
            return pl.ds(pl.multiple_of((pair_id ^ bits) * rows, 64), rows)

        own_copy = pltpu.make_async_copy(own, a_ref.at[at(0)], sems.at[0])
        own_copy.start()
        coupling_copy = pltpu.make_async_copy(c_hbm, c_ref, sems.at[1])
        coupling_copy.start()
        half = blocks // 2
        width = half * LEAF
        there = pl.ds(pl.multiple_of((1 - pair_id // 2) * width, LEAF), width)
        a_ref[at(1), :] = near[...]
        a_ref[at(2), there] = far[...]
        a_ref[at(3), there] = cross[...]
        own_copy.wait()

        @pl.when(pair_id >= 2)
        def _():
            for i in range(half, blocks):
                for j in range(half):
                    low, high = span(i, i + 1), span(j, j + 1)
                    a_ref[high, low] = a_ref[low, high].T

        earlier = []
    else:
        a_ref, c_ref = refs[:2]
        earlier = refs[2 : 2 + 6 * index]
        outs = refs[2 + 6 * index : 2 + 6 * index + n_out]
        d_ref, x_ref = refs[2 + 6 * index + n_out :]
    uppers, lowers, panels = [], [], []
    for i in range(index):
        p_high, p_low, u_high, u_low, l_high, l_low = earlier[6 * i : 6 * i + 6]
        panels.append((stages[i], (p_high, p_low)))
        uppers.append((stages[i], (u_high, u_low)))
        lowers.append((stages[i], (l_high, l_low)))
    panel_ref, p_high, p_low = outs[:3]
    panels.append((leaves, (p_high, p_low)))
    if keep:
        uppers.append((leaves, outs[3:5]))
        lowers.append((leaves, outs[5:7]))
    uppers, lowers, panels = Columns(uppers, 0), Columns(lowers, 1), Columns(panels, 1)
    every = slice(None)
    for slot, k in enumerate(leaves):
        here, rest = span(k, k + 1), span(k + 1, blocks)
        diag = a_ref[here, here]
        if k:
            diag = diag - three(lowers.get(k, here), uppers.get(k, here))
        d_ref[slot] = diag
        side = None
        if k and k + 1 < blocks:
            side = a_ref[here, rest] - three(lowers.get(k, here), uppers.get(k, rest))
        elif k + 1 < blocks:
            side = a_ref[here, rest]
        if k:
            coupled = c_ref[:, here] - three(panels.get(k, every), uppers.get(k, here))
        factor_leaf(d_ref.at[slot], x_ref.at[slot])
        inverse = x_ref[slot]
        if index == 0:
            inverse_ref[slot] = inverse
        if k == 0:
            coupling_copy.wait()
            coupled = c_ref[:, here]
        if side is not None:
            upper = three(halves(inverse), halves(side))
            uppers.put(k, rest, upper)
            for j in range(k + 1, blocks):
                lowers.put(k, span(j, j + 1), upper[:, span(j - k - 1, j - k)].T)
        panel = three(halves(coupled), halves(inverse.T))
        panel_ref[:, span(slot, slot + 1)] = panel
        panels.put(k, every, panel)


def stage(stages, index, blocks, operands, upd_rows, piv):
    width = len(stages[index]) * LEAF
    first, keep = index == 0, stages[index][0] + 1 < blocks
    shapes = [((upd_rows, width), F32)] + [((upd_rows, width), BF16)] * 2
    if keep:
        shapes += [((width, piv), BF16)] * 2 + [((piv, width), BF16)] * 2
    scratch = [pltpu.VMEM((len(stages[index]), LEAF, LEAF), F32)] * 2
    in_specs = [VMEM] * len(operands)
    if first:
        shapes += [((piv, piv), F32), ((upd_rows, piv), F32)]
        shapes += [((len(stages[0]), LEAF, LEAF), F32)]
        scratch.append(pltpu.SemaphoreType.DMA((2,)))
        in_specs = [HBM, VMEM, VMEM, VMEM, HBM]
        operands = [in_hbm(operands[0]), *operands[1:4], in_hbm(operands[4])]
    return pl.pallas_call(
        functools.partial(stage_kernel, stages, index, blocks),
        out_shape=[jax.ShapeDtypeStruct(*shape) for shape in shapes],
        in_specs=in_specs,
        out_specs=[VMEM] * len(shapes),
        scratch_shapes=scratch,
        cost_estimate=pl.CostEstimate(
            flops=len(stages[index]) * 2000000000, bytes_accessed=1 << 20, transcendentals=0
        ),
        compiler_params=pltpu.CompilerParams(vmem_limit_bytes=20 << 20),
    )(*operands)


def run_stages(parts, coupling, after_stage):
    upd_rows, piv = coupling.shape
    blocks = piv // LEAF
    columns, operands, base, earlier = [], [*parts, coupling], None, []
    for index in range(len(STAGES)):
        outs = stage(STAGES, index, blocks, operands, upd_rows, piv)
        columns.append(outs[0])
        after_stage(index, outs)
        if index == 0:
            base = outs[7:9]
        earlier += outs[1:7]
        operands = [*base, *earlier]
    return columns


STAGES = ((0, 1, 2), (3, 4), (5,))


LATE = 2
FIRST = 3


def place_panels(sources, all_ref, at):
    pair_id = lax.axis_index("pair")
    width = sources[0].shape[1]
    for bits, source in enumerate(sources):
        all_ref[pair_id ^ bits, :, at : at + width] = source[...]


def gram(left, right):
    return lax.dot_general(left, right, (((1,), (1,)), ((), ())), preferred_element_type=F32)


def partial_kernel(ahead, *refs):
    t_ref, own_ref, near, far, cross, inverse_ref, u_high, u_low, *sources, w_ref, all_ref = refs
    pair_id = lax.axis_index("pair")
    width = own_ref.shape[1]
    all_ref[pair_id, :, :width] = own_ref[...]
    leaves = width // LEAF
    solved = [[jnp.zeros((LEAF, LEAF), F32)] * leaves for _ in range(leaves)]
    for k in range(leaves):
        solved[k][k] = inverse_ref[k].T
        for j in range(k):
            total = 0.0
            for i in range(j, k):
                at = span(i, i + 1), span(k, k + 1)
                total = total + three(halves(solved[j][i]), (u_high[at], u_low[at]))
            solved[j][k] = -three(halves(total), halves(solved[k][k]))
    whole = halves(jnp.concatenate([jnp.concatenate(row, 1) for row in solved], 0))
    tile = own_ref.shape[0] // 4

    def panel_rows(i, _):
        rows = pl.ds(pl.multiple_of(i * tile, 16), tile)
        for bits, early in ((1, near), (2, far), (3, cross)):
            panel = three(halves(early[rows, :]), whole)
            all_ref[pair_id ^ bits, rows, :width] = panel.astype(BF16)
        return 0

    lax.fori_loop(0, 4, panel_rows, 0)
    at = width
    for chunk in range(len(sources) // 4):
        four = sources[4 * chunk : 4 * chunk + 4]
        place_panels(four, all_ref, at)
        at += four[0].shape[1]
    sibling = lax.rem(lax.axis_index("front"), 4)
    upd_rows = t_ref.shape[0]

    def rows_of(i, _):
        rows = pl.ds(pl.multiple_of(i * tile, 16), tile)
        own = [own_ref[rows, :]] + [sources[i][rows, :] for i in range(0, len(sources), 4)]
        own = jnp.concatenate(own, 1)
        for column in range(4):

            @pl.when((sibling == column ^ FIRST) == ahead)
            def _():
                trailing = t_ref[rows, column * upd_rows : (column + 1) * upd_rows]
                w_ref[sibling ^ column, rows, :] = trailing - gram(own, all_ref[column])

        return 0

    lax.fori_loop(0, 4, rows_of, 0)


def partial_update(trailing, first, early, chunks, ahead):
    upd_rows = trailing.shape[0]
    width = first[1].shape[1] + sum(chunk[0].shape[1] for chunk in chunks)
    start = [trailing, first[1], *early[1:], first[9], first[3], first[4]]
    sources = [source for chunk in chunks for source in chunk]
    return pl.pallas_call(
        functools.partial(partial_kernel, ahead),
        out_shape=jax.ShapeDtypeStruct((4, upd_rows, upd_rows), F32),
        in_specs=[VMEM] * (len(start) + len(sources)),
        out_specs=VMEM,
        scratch_shapes=[pltpu.VMEM((4, upd_rows, width), BF16)],
        cost_estimate=pl.CostEstimate(flops=8000000000, bytes_accessed=1 << 20, transcendentals=0),
        compiler_params=pltpu.CompilerParams(vmem_limit_bytes=24 << 20),
    )(*start, *sources)


def finish_kernel(bits, n_sources, w_ref, *refs):
    sources, refs = refs[:n_sources], refs[n_sources:]
    copies = []
    if bits == 0:
        columns, (u_ref, f_ref, all_ref, sems) = refs[:-4], refs[-4:]
        at = 0
        for i, column in enumerate(columns):
            width = column.shape[1]
            copies.append(pltpu.make_async_copy(column, f_ref.at[:, at : at + width], sems.at[i]))
            copies[-1].start()
            at += width
    else:
        u_ref, all_ref = refs
    at = 0
    for first in range(0, n_sources, 4):
        place_panels(sources[first : first + 4], all_ref, at)
        at += sources[first].shape[1]
    own = jnp.concatenate([sources[i][...] for i in range(0, n_sources, 4)], 1)
    sibling = lax.rem(lax.axis_index("front"), 4)
    u_ref[...] = (w_ref[bits] - gram(own, all_ref[sibling ^ bits])).astype(BF16)
    for copy in copies:
        copy.wait()


def finish_update(partial, chunks, bits, columns=()):
    upd_rows = partial.shape[1]
    sources = [source for chunk in chunks for source in chunk]
    width = sum(chunk[0].shape[1] for chunk in chunks)
    shapes = [jax.ShapeDtypeStruct((upd_rows, upd_rows), BF16)]
    out_specs = [VMEM]
    scratch = [pltpu.VMEM((4, upd_rows, width), BF16)]
    if columns:
        piv = sum(column.shape[1] for column in columns)
        shapes.append(jax.ShapeDtypeStruct((upd_rows, piv), F32))
        out_specs.append(HBM)
        scratch.append(pltpu.SemaphoreType.DMA((len(columns),)))
    return pl.pallas_call(
        functools.partial(finish_kernel, bits, len(sources)),
        out_shape=shapes,
        in_specs=[VMEM] * (1 + len(sources) + len(columns)),
        out_specs=out_specs,
        scratch_shapes=scratch,
        cost_estimate=pl.CostEstimate(flops=500000000, bytes_accessed=1 << 20, transcendentals=0),
        compiler_params=pltpu.CompilerParams(vmem_limit_bytes=12 << 20),
    )(partial, *sources, *columns)


def hot_block(map_ref, block, upd_rows):
    low = max(0, (block - 2) * LEAF)
    high = min((block + 1) * LEAF, upd_rows)
    rows = lax.broadcasted_iota(jnp.int32, (LEAF, high - low), 0) + block * LEAF
    return (rows == map_ref[:, low:high]).astype(F32).astype(BF16), low, high


def extend_kernel(first, last, *refs):
    part_ref, row_ref, col_ref = refs[:3]
    refs = refs[3:]
    if not first:
        sum_ref, refs = refs[0], refs[1:]
    if last:
        out_ref, moved_ref, flat_ref, sems = refs
    else:
        out_ref, moved_ref = refs
    upd_rows = part_ref.shape[0]
    blocks = moved_ref.shape[1] // LEAF
    for j in range(blocks):
        hot, low, high = hot_block(col_ref, j, upd_rows)
        moved_ref[:, j * LEAF : (j + 1) * LEAF] = lax.dot_general(
            part_ref[:, low:high], hot, (((1,), (1,)), ((), ())), preferred_element_type=F32
        ).astype(BF16)
    copies = []
    for i in range(blocks):
        rows = slice(i * LEAF, (i + 1) * LEAF)
        hot, low, high = hot_block(row_ref, i, upd_rows)
        value = jnp.dot(hot, moved_ref[low:high, :], preferred_element_type=F32)
        if not first:
            value = value + sum_ref[rows, :]
        if last:
            flat_ref[rows, 0, :] = value
            copy = pltpu.make_async_copy(flat_ref.at[rows], out_ref.at[rows], sems.at[i])
            copy.start()
            copies.append(copy)
        else:
            out_ref[rows, :] = value
    for copy in copies:
        copy.wait()


def extend_add(total, part, row_map, col_map, par_rows, last):
    first = total is None
    upd_rows = part.shape[0]
    scratch = [pltpu.VMEM((upd_rows, par_rows), BF16)]
    shape, out_specs = (par_rows, par_rows), pl.BlockSpec(memory_space=pltpu.VMEM)
    if last:
        shape, out_specs = (par_rows, 1, par_rows), HBM
        scratch += [
            pltpu.VMEM((par_rows, 1, par_rows), F32),
            pltpu.SemaphoreType.DMA((par_rows // LEAF,)),
        ]
    operands = [part, row_map, col_map] + ([] if first else [total])
    return pl.pallas_call(
        functools.partial(extend_kernel, first, last),
        out_shape=jax.ShapeDtypeStruct(shape, F32),
        in_specs=[pl.BlockSpec(memory_space=pltpu.VMEM)] * len(operands),
        out_specs=out_specs,
        scratch_shapes=scratch,
        input_output_aliases={} if first or last else {3: 0},
        cost_estimate=pl.CostEstimate(
            flops=2 * upd_rows * par_rows * par_rows, bytes_accessed=1 << 20, transcendentals=0
        ),
        compiler_params=pltpu.CompilerParams(vmem_limit_bytes=24 << 20),
    )(*operands)


def level(pivot_block, coupling_rows, trailing_block, index_map):
    child_id = lax.axis_index("front")
    pair_id = lax.axis_index("pair")
    pairs = lax.axis_size("pair")
    sibling = child_id % 4
    upd_rows = coupling_rows.shape[1]
    par_rows = PO // pairs
    parts = gather_pivot(pivot_block[0], pair_id)
    early = coupling_rows[0, :, : len(STAGES[0]) * LEAF]
    early = gather_pair(early)
    chunks, firsts = [], []

    def after_stage(index, outs):
        if index == 0:
            firsts.append(outs)
        else:
            chunks.append(gather_pair(outs[1]))

    columns = run_stages(parts, coupling_rows[0], after_stage)
    ahead = partial_update(trailing_block[0], firsts[0], early, chunks[:-LATE], True)
    others = partial_update(trailing_block[0], firsts[0], early, chunks[:-LATE], False)

    def local_map(which, block):
        own = lax.dynamic_slice(index_map, (which, block * upd_rows), (1, upd_rows))
        return own - block * par_rows

    maps = [
        (local_map(child_id ^ bits, pair_id), local_map(child_id ^ bits, sibling))
        for bits in range(4)
    ]
    parts = {}
    for bits in (FIRST, 1, 2):
        partial = ahead if bits == FIRST else others
        (update,) = finish_update(partial, chunks[-LATE:], bits)
        parts[bits] = xor_permute(update, "front", bits)
    parts[0], factor = finish_update(others, chunks[-LATE:], 0, columns)
    assembled = None
    for bits in (0, 3, 1, 2):
        assembled = extend_add(assembled, parts[bits], *maps[bits], par_rows, bits == 2)
    return (factor[None, :, :], assembled)


def solution(mesh):
    in_specs = (P("front", "pair", None), P("front", "pair", None), P("front", "pair", None), P())
    out_specs = (P("front", "pair", None), P("pair", "front", None))
    return jax.shard_map(level, mesh=mesh, in_specs=in_specs, out_specs=out_specs, check_vma=False)
```
